32 devices in a mesh: dp: 8 (over y, x, core), tensor: 4 (over z).
Axes of the slice: x: 2, y: 2, z: 4, core: 2. Of those that a mesh axis runs over, the one named last changes fastest.
Arguments:
- inputs: float32 [4096, 768], P(('dp', 'tensor')), may hold values from -6 to 6
- qkv_weight: bfloat16 [1, 768, 3, 768], P(None, 'dp', None, 'tensor'), as said below
- out_weight: bfloat16 [1, 768, 768], P(None, 'tensor', 'dp'), may hold values from -1.75 to 1.75
- fc_weight: bfloat16 [1, 768, 3072], P(None, 'dp', 'tensor'), may hold values from -0.21875 to 0.21875
- proj_weight: bfloat16 [1, 3072, 768], P(None, 'tensor', 'dp'), may hold values from -0.109375 to 0.109375
- vectors: float32 [1, 12, 768], P(None, None, ('dp', 'tensor')), as said below
- out_grad: float32 [4096, 768], P(('dp', 'tensor')), may hold values from -6 to 6
Outputs:
- outputs: float32 [4096, 768], P(('dp', 'tensor'))
- input_grad: float32 [4096, 768], P(('dp', 'tensor'))
- qkv_grad: float32 [1, 768, 3, 768], P(None, 'dp', None, 'tensor')
- out_weight_grad: float32 [1, 768, 768], P(None, 'tensor', 'dp')
- fc_grad: float32 [1, 768, 3072], P(None, 'dp', 'tensor')
- proj_grad: float32 [1, 3072, 768], P(None, 'tensor', 'dp')
- vector_grad: float32 [1, 12, 768], P(None, None, ('dp', 'tensor'))
The draws below stay inside these ranges and needn't reach their ends.
Inputs may be any that keep to these rules, and one draw needn't show every extreme that they name: `vectors`: gains lie near one, biases are of order 0.3. `qkv_weight`: entries are of order D ** -0.5.
All inputs are finite; a program needn't handle non-finite values.
Results may differ from the reference program's by a relative error of at most 0.018.
Values may be sent and summed in bfloat16 or wider, within the bound.
No kernel may reach another device: no remote copies, remote signals or barrier semaphores. Data moves between devices by JAX's collectives and lax.ppermute only.
A program may use at most 64 MiB of HBM per device.

```python
import math
import jax
import jax.numpy as jnp
from jax import lax

D = 768
HEADS = 12
HEAD_DIM = 64
FF = 3072
LAYERS = 1
SEQ_LEN = 256
VEC_ROWS = 12
TOKENS = 4096


def draw_qkv_weight(key, part):
    keys = jax.random.split(key, 1)
    shape = (LAYERS, D, 3, D)
    base = jax.random.truncated_normal(keys[0], -4.0, 4.0, shape, jnp.float32)
    return (base * D ** (-0.5)).astype(jnp.bfloat16)


def draw_vectors(key, part):
    keys = jax.random.split(key, 2)
    shape = (LAYERS, VEC_ROWS, D)
    noise = jax.random.normal(keys[1], shape, jnp.float32)
    rows = jnp.arange(VEC_ROWS)[None, :, None]
    is_gain = (rows == 0) | (rows == 5)
    gains = 1.0 + 0.3 * jnp.clip(noise, -1.5, 1.5)
    biases = 0.3 * jnp.clip(noise, -3.0, 3.0)
    return jnp.where(is_gain, gains, biases)


def spiked(drawn, own_key, source, target, blocks, factor):
    owner, partner = [(jnp.arange(drawn.shape[dim]) // (drawn.shape[dim] // blocks)).reshape([-1 if axis == dim else 1 for axis in range(drawn.ndim)]) for dim in (source, target)]
    chosen = jax.random.permutation(own_key, blocks)[partner]
    strong = (owner == chosen) | (owner == (partner + blocks // 2) % blocks)
    return jnp.where(strong, factor * drawn, drawn)


def level_of(own_key, dims, cuts, smallest, top_value):
    level, own = 1.0, jax.random.fold_in(own_key, 6)
    for position, parts in cuts:
        draws = jnp.exp(jax.random.uniform(jax.random.fold_in(own, position), (parts,), jnp.float32, smallest / len(cuts), top_value / len(cuts)))
        level = level * jnp.repeat(draws, dims[position] // parts).reshape([-1 if axis == position else 1 for axis in range(len(dims))])
    return level


def normal_values(key, dims, scale, bound, pieces=(), kind=jnp.bfloat16):
    values = jax.random.normal(key, dims, jnp.float32) * scale
    if len(pieces) > 0:
        values = level_of(key, dims, pieces, -0.22, 0.18) * values
    return jnp.clip(values, min=-bound, max=bound).astype(kind)


def bell_draw_with(own_key, shape, scale, limit, cuts, heavy, kind=jnp.bfloat16):
    array = scale * jax.random.normal(own_key, shape, jnp.float32)
    if cuts:
        array = array * level_of(own_key, shape, cuts, -0.22, 0.18)
    return jnp.clip(spiked(array, jax.random.fold_in(own_key, 3), *heavy), -limit, limit).astype(kind)


def setup_inputs(seed: int = 0) -> dict:
    key_list = jax.random.split(jax.random.key(seed), 8)
    inputs = normal_values(key_list[0], (TOKENS, D), 1.0, 6.0, ((0, 32),), jnp.float32)
    qkv_weight = draw_qkv_weight(jax.random.fold_in(key_list[7], 71), 0)
    out_weight = normal_values(key_list[2], (LAYERS, D, D), (max(D // 64, 4)) ** -0.5, 1.75, ((1, 4), (2, 8)))
    fc_weight = normal_values(key_list[3], (LAYERS, D, FF), D ** -0.5, 0.21875, ((1, 8), (2, 4)))
    proj_weight = normal_values(key_list[4], (LAYERS, FF, D), FF ** -0.5, 0.109375, ((1, 4), (2, 8)))
    vectors = draw_vectors(jax.random.fold_in(key_list[7], 71), 0)
    out_grad = bell_draw_with(key_list[6], (TOKENS, D), 1.0, 6.0, ((0, 32),), (0, 1, 32, 2.75), jnp.float32)
    return dict(inputs=inputs, qkv_weight=qkv_weight, out_weight=out_weight, fc_weight=fc_weight, proj_weight=proj_weight, vectors=vectors, out_grad=out_grad)


NORM_EPS = 1e-05
GELU_COEF = 0.7978845608028654
MASK_LOW = -1000000000.0

def layer_norm(rows, gain, shift):
    mean = lax.optimization_barrier(jnp.mean(rows, axis=-1, keepdims=True))
    centred = rows - mean
    variance = lax.optimization_barrier(jnp.mean(centred * centred, axis=-1, keepdims=True))
    inv_std = lax.rsqrt(variance + NORM_EPS)
    normed = centred * inv_std
    return (normed * gain + shift, normed, inv_std)

def layer_norm_back(grad_out, normed, inv_std, gain):
    grad_normed = grad_out * gain
    mean_one = lax.optimization_barrier(jnp.mean(grad_normed, axis=-1, keepdims=True))
    mean_two = lax.optimization_barrier(jnp.mean(grad_normed * normed, axis=-1, keepdims=True))
    grad_rows = inv_std * (grad_normed - mean_one - normed * mean_two)
    return (grad_rows, lax.optimization_barrier(jnp.sum(grad_out * normed, 0)), lax.optimization_barrier(jnp.sum(grad_out, 0)))

def gelu_parts(pre):
    inner = GELU_COEF * (pre + 0.044715 * pre * pre * pre)
    tanh_val = jnp.tanh(inner)
    value = 0.5 * pre * (1.0 + tanh_val)
    slope = 0.5 * (1.0 + tanh_val) + 0.5 * pre * (1.0 - tanh_val * tanh_val) * GELU_COEF * (1.0 + 3.0 * 0.044715 * pre * pre)
    return (value, slope)

def causal_mask(length):
    rows = lax.broadcasted_iota(jnp.int32, (length, length), 0)
    cols = lax.broadcasted_iota(jnp.int32, (length, length), 1)
    return rows >= cols

def attend(query, keys, values):
    scale = HEAD_DIM ** (-0.5)
    scores = jnp.einsum('qhd,khd->hqk', query.astype(jnp.float32), keys.astype(jnp.float32)) * scale
    scores = jnp.where(causal_mask(query.shape[0])[None], scores, MASK_LOW)
    top = lax.optimization_barrier(jnp.max(scores, axis=-1, keepdims=True))
    total = lax.optimization_barrier(jnp.sum(jnp.exp(scores - top), axis=-1, keepdims=True))
    log_total = top + jnp.log(total)
    probs = jnp.exp(scores - log_total).astype(jnp.bfloat16)
    context = jnp.einsum('hqk,khd->qhd', probs.astype(jnp.float32), values.astype(jnp.float32)).astype(jnp.bfloat16)
    return (context, log_total)

def attend_back(query, keys, values, log_total, grad_ctx):
    scale = HEAD_DIM ** (-0.5)
    scores = jnp.einsum('qhd,khd->hqk', query.astype(jnp.float32), keys.astype(jnp.float32)) * scale
    scores = jnp.where(causal_mask(query.shape[0])[None], scores, MASK_LOW)
    probs = jnp.exp(scores - log_total)
    probs_low = probs.astype(jnp.bfloat16)
    grad_ctx32 = grad_ctx.astype(jnp.float32)
    grad_values = jnp.einsum('hqk,qhd->khd', probs_low.astype(jnp.float32), grad_ctx32)
    grad_probs = jnp.einsum('qhd,khd->hqk', grad_ctx32, values.astype(jnp.float32))
    row_sum = lax.optimization_barrier(jnp.sum(probs * grad_probs, axis=-1, keepdims=True))
    grad_scores = (probs * (grad_probs - row_sum) * scale).astype(jnp.bfloat16).astype(jnp.float32)
    grad_query = jnp.einsum('hqk,khd->qhd', grad_scores, keys.astype(jnp.float32))
    grad_keys = jnp.einsum('hqk,qhd->khd', grad_scores, query.astype(jnp.float32))
    return (grad_query, grad_keys, grad_values)

def block_pass(x_rows, grad_rows, qkv_weight, out_weight, fc_weight, proj_weight, vectors):
    count = x_rows.shape[0]
    seq_count = count // SEQ_LEN
    saved = []
    resid = x_rows
    for layer in range(LAYERS):
        vec = vectors[layer]
        w_qkv = qkv_weight[layer].reshape(D, 3 * D)
        w_out = out_weight[layer]
        w_fc = fc_weight[layer]
        w_proj = proj_weight[layer]
        normed_out, normed1, inv1 = layer_norm(resid, vec[0], vec[1])
        a_rows = normed_out.astype(jnp.bfloat16)
        qkv = jnp.dot(a_rows, w_qkv, preferred_element_type=jnp.float32).reshape(count, 3, D)
        query = (qkv[:, 0] + vec[2]).astype(jnp.bfloat16).reshape(seq_count, SEQ_LEN, HEADS, HEAD_DIM)
        keys = qkv[:, 1].astype(jnp.bfloat16).reshape(seq_count, SEQ_LEN, HEADS, HEAD_DIM)
        values = (qkv[:, 2] + vec[3]).astype(jnp.bfloat16).reshape(seq_count, SEQ_LEN, HEADS, HEAD_DIM)
        context, log_total = jax.vmap(attend)(query, keys, values)
        ctx_flat = context.reshape(count, D)
        resid1 = resid + jnp.dot(ctx_flat, w_out, preferred_element_type=jnp.float32) + vec[4]
        normed_out2, normed2, inv2 = layer_norm(resid1, vec[5], vec[6])
        m_rows = normed_out2.astype(jnp.bfloat16)
        bias_fc = vec[8:].reshape(FF)
        pre = jnp.dot(m_rows, w_fc, preferred_element_type=jnp.float32) + bias_fc
        act, slope = gelu_parts(pre)
        act_low = act.astype(jnp.bfloat16)
        resid = resid1 + jnp.dot(act_low, w_proj, preferred_element_type=jnp.float32) + vec[7]
        saved.append((a_rows, normed1, inv1, query, keys, values, log_total, ctx_flat, normed2, inv2, m_rows, slope, act_low))
    outputs = resid
    grad = grad_rows
    grads = [None] * LAYERS
    for layer in reversed(range(LAYERS)):
        vec = vectors[layer]
        w_qkv = qkv_weight[layer].reshape(D, 3 * D)
        w_out = out_weight[layer]
        w_fc = fc_weight[layer]
        w_proj = proj_weight[layer]
        a_rows, normed1, inv1, query, keys, values, log_total, ctx_flat, normed2, inv2, m_rows, slope, act_low = saved[layer]
        g_bias_proj = lax.optimization_barrier(jnp.sum(grad, 0))
        grad_low = grad.astype(jnp.bfloat16)
        g_proj = jnp.dot(act_low.T, grad_low, preferred_element_type=jnp.float32)
        d_pre = jnp.dot(grad_low, w_proj.T, preferred_element_type=jnp.float32) * slope
        g_bias_fc = lax.optimization_barrier(jnp.sum(d_pre, 0))
        d_pre_low = d_pre.astype(jnp.bfloat16)
        g_fc = jnp.dot(m_rows.T, d_pre_low, preferred_element_type=jnp.float32)
        d_m = jnp.dot(d_pre_low, w_fc.T, preferred_element_type=jnp.float32)
        d_in, g_gain2, g_shift2 = layer_norm_back(d_m, normed2, inv2, vec[5])
        grad1 = grad + d_in
        g_bias_out = lax.optimization_barrier(jnp.sum(grad1, 0))
        grad1_low = grad1.astype(jnp.bfloat16)
        g_out = jnp.dot(ctx_flat.T, grad1_low, preferred_element_type=jnp.float32)
        d_ctx = jnp.dot(grad1_low, w_out.T, preferred_element_type=jnp.float32).astype(jnp.bfloat16)
        d_ctx = d_ctx.reshape(count // SEQ_LEN, SEQ_LEN, HEADS, HEAD_DIM)
        d_query, d_keys, d_values = jax.vmap(attend_back)(query, keys, values, log_total, d_ctx)
        d_query = d_query.reshape(count, D)
        d_keys = d_keys.reshape(count, D)
        d_values = d_values.reshape(count, D)
        g_bias_q = lax.optimization_barrier(jnp.sum(d_query, 0))
        g_bias_v = lax.optimization_barrier(jnp.sum(d_values, 0))
        d_qkv = jnp.stack([d_query, d_keys, d_values], axis=1).astype(jnp.bfloat16).reshape(count, 3 * D)
        g_qkv = jnp.dot(a_rows.T, d_qkv, preferred_element_type=jnp.float32).reshape(D, 3, D)
        d_a = jnp.dot(d_qkv, w_qkv.T, preferred_element_type=jnp.float32)
        d_in1, g_gain1, g_shift1 = layer_norm_back(d_a, normed1, inv1, vec[0])
        grad = grad1 + d_in1
        head_rows = jnp.stack([g_gain1, g_shift1, g_bias_q, g_bias_v, g_bias_out, g_gain2, g_shift2, g_bias_proj])
        vec_grad = jnp.concatenate([head_rows, g_bias_fc.reshape(FF // D, D)], axis=0)
        grads[layer] = (g_qkv, g_out, g_fc, g_proj, vec_grad)
    stacked = tuple((jnp.stack([grads[i][j] for i in range(LAYERS)]) for j in range(5)))
    return (outputs, grad, stacked)

def reference(inputs, qkv_weight, out_weight, fc_weight, proj_weight, vectors, out_grad):
    seq_total = TOKENS // SEQ_LEN
    group = math.gcd(seq_total, 8)
    blocks = seq_total // group
    x_blocks = inputs.reshape(blocks, group * SEQ_LEN, D)
    g_blocks = out_grad.reshape(blocks, group * SEQ_LEN, D)
    init = (jnp.zeros((LAYERS, D, 3, D), jnp.float32), jnp.zeros((LAYERS, D, D), jnp.float32), jnp.zeros((LAYERS, D, FF), jnp.float32), jnp.zeros((LAYERS, FF, D), jnp.float32), jnp.zeros((LAYERS, VEC_ROWS, D), jnp.float32))

    def step(carry, pair):
        outs, grad_in, grads = block_pass(pair[0], pair[1], qkv_weight, out_weight, fc_weight, proj_weight, vectors)
        return (tuple((c + g for c, g in zip(carry, grads))), (outs, grad_in))
    totals, (outs, grad_ins) = lax.scan(step, init, (x_blocks, g_blocks))
    return (outs.reshape(TOKENS, D), grad_ins.reshape(TOKENS, D), totals[0], totals[1], totals[2], totals[3], totals[4])
```

```python
import jax
import jax.numpy as jnp
from jax import lax
from jax.experimental import pallas as pl
from jax.experimental.pallas import tpu as pltpu
from jax.sharding import PartitionSpec as P

HEAD_DIM = 64
SEQ_LEN = 256
NORM_EPS = 1e-05
GELU_COEF = 0.7978845608028654
MASK_LOW = -1000000000.0
F32 = jnp.float32
BF16 = jnp.bfloat16
TP = 4


def mm(a, b, ca=1, cb=0):
    return lax.dot_general(a, b, (((ca,), (cb,)), ((), ())), preferred_element_type=F32)


def norm_rows(rows):
    mean = jnp.mean(rows, axis=-1, keepdims=True)
    centred = rows - mean
    variance = jnp.mean(centred * centred, axis=-1, keepdims=True)
    inv_std = lax.rsqrt(variance + NORM_EPS)
    return centred * inv_std, inv_std


def norm_back(grad_out, normed, inv_std, gain):
    grad_normed = grad_out * gain
    mean_one = jnp.mean(grad_normed, axis=-1, keepdims=True)
    mean_two = jnp.mean(grad_normed * normed, axis=-1, keepdims=True)
    return inv_std * (grad_normed - mean_one - normed * mean_two)


def gelu_parts(pre):
    inner = GELU_COEF * (pre + 0.044715 * pre * pre * pre)
    tanh_val = jnp.tanh(inner)
    value = 0.5 * pre * (1.0 + tanh_val)
    slope = 0.5 * (1.0 + tanh_val) + 0.5 * pre * (1.0 - tanh_val * tanh_val) * GELU_COEF * (
        1.0 + 3.0 * 0.044715 * pre * pre
    )
    return (value, slope)


def call(body, outs, scalars=None, name=None, scratch=()):
    def run(*args):
        specs = [pl.BlockSpec(memory_space=pltpu.VMEM)] * len(args)
        if scalars is not None:
            specs = [pl.BlockSpec(memory_space=pltpu.SMEM)] + specs
            args = (scalars,) + args
        return pl.pallas_call(
            body,
            out_shape=[jax.ShapeDtypeStruct(s, d) for s, d in outs],
            in_specs=specs,
            out_specs=[pl.BlockSpec(memory_space=pltpu.VMEM)] * len(outs),
            scratch_shapes=list(scratch),
            name=name,
        )(*args)

    return run


def first_body(x_ref, g_ref, xhat_ref, dy_ref):
    normed, _ = norm_rows(x_ref[...])
    xhat_ref[...] = normed.astype(BF16)
    dy_ref[...] = g_ref[...].astype(BF16)


def pick(vec, row, part, cols):
    out = jnp.zeros((1, cols), F32)
    for p in range(TP):
        out = jnp.where(part == p, vec[row : row + 1, p * cols : (p + 1) * cols], out)
    return out


def put_parts(refs, s, value):
    refs[s][...] = value.astype(refs[s].dtype)


def time_mask(flip):
    rows = lax.broadcasted_iota(jnp.int32, (SEQ_LEN, SEQ_LEN), 0)
    cols = lax.broadcasted_iota(jnp.int32, (SEQ_LEN, SEQ_LEN), 1)
    shift = flip * (SEQ_LEN // 2)
    return (rows ^ shift) >= (cols ^ shift)


def attn_fwd_body(sc, x0, x1, x2, x3, wa, vec, a_ref, q_ref, k_ref, v_ref, lse_ref, ctx_ref, *parts):
    part, flip = sc[0], sc[1]
    cols = q_ref.shape[1]
    block = x0.shape[0]
    table = vec[...]
    for s, ref in enumerate((x0, x1, x2, x3)):
        a_ref[s * block : (s + 1) * block, :] = (
            ref[...].astype(F32) * table[0:1] + table[1:2]
        ).astype(BF16)
    qkv = mm(a_ref[...], wa[:, : 3 * cols])
    q_ref[...] = (qkv[:, :cols] + pick(table, 2, part, cols)).astype(BF16)
    k_ref[...] = qkv[:, cols : 2 * cols].astype(BF16)
    v_ref[...] = (qkv[:, 2 * cols :] + pick(table, 3, part, cols)).astype(BF16)
    mask = time_mask(flip)
    for seq in range(q_ref.shape[0] // SEQ_LEN):
        rows = slice(seq * SEQ_LEN, (seq + 1) * SEQ_LEN)
        for h in range(cols // HEAD_DIM):
            lanes = slice(h * HEAD_DIM, (h + 1) * HEAD_DIM)
            s = mm(q_ref[rows, lanes], k_ref[rows, lanes], 1, 1) * HEAD_DIM ** (-0.5)
            s = jnp.where(mask, s, MASK_LOW)
            top = jnp.max(s, axis=-1, keepdims=True)
            e = jnp.exp(s - top)
            total = jnp.sum(e, axis=-1, keepdims=True)
            lse_ref[rows, h : h + 1] = top + jnp.log(total)
            p = (e * (1.0 / total)).astype(BF16)
            ctx_ref[rows, lanes] = mm(p, v_ref[rows, lanes]).astype(BF16)
    out = mm(ctx_ref[...], wa[:, 3 * cols :], 1, 1)
    for s in range(TP):
        put_parts(parts, s, out[s * block : (s + 1) * block])


def norm2_body(x_ref, p0, r1, r2, r3, vec, resid_ref, m_ref):
    got = r1[...].astype(F32) + r2[...].astype(F32) + r3[...].astype(F32)
    resid = x_ref[...] + (p0[...] + got) + vec[4:5, :]
    resid_ref[...] = resid
    normed, _ = norm_rows(resid)
    m_ref[...] = (normed * vec[5:6, :] + vec[6:7, :]).astype(BF16)


def mlp_body(sc, m0, m1, m2, m3, d0, d1, d2, d3, wb, vec, h_ref, du_ref, gbf_ref, *parts):
    part = sc[0]
    hid = h_ref.shape[1]
    block = m0.shape[0]
    bias = vec[pl.ds(8 + part, 1), :]
    total = jnp.zeros((1, hid), F32)
    for s, (m, d) in enumerate(((m0, d0), (m1, d1), (m2, d2), (m3, d3))):
        rows = slice(s * block, (s + 1) * block)
        act, slope = gelu_parts(mm(m[...], wb[:, :hid]) + bias)
        h_ref[rows, :] = act.astype(BF16)
        du = mm(d[...], wb[:, hid:]) * slope
        total = total + jnp.sum(du, axis=0, keepdims=True)
        du_ref[rows, :] = du.astype(BF16)
    gbf_ref[...] = total
    for s in range(TP):
        rows = slice(s * block, (s + 1) * block)
        put_parts(parts[TP:], s, mm(du_ref[rows, :], wb[:, :hid], 1, 1))
        put_parts(parts[:TP], s, mm(h_ref[rows, :], wb[:, hid:], 1, 1))


def mlp_grad_body(m0, m1, m2, m3, d0, d1, d2, d3, h_ref, du_ref, g_ref):
    hid = h_ref.shape[1]
    m = jnp.concatenate([m0[...], m1[...], m2[...], m3[...]], axis=0)
    g_ref[:, :hid] = mm(m, du_ref[...], 0, 0).astype(BF16)
    d = jnp.concatenate([d0[...], d1[...], d2[...], d3[...]], axis=0)
    g_ref[:, hid:] = mm(d, h_ref[...], 0, 0).astype(BF16)


def norm2_back_body(resid_ref, p0, r1, r2, r3, grad_ref, vec, dr_ref, dz_ref, sums_ref):
    d_m = p0[...] + (r1[...].astype(F32) + r2[...].astype(F32) + r3[...].astype(F32))
    normed, inv_std = norm_rows(resid_ref[...])
    grad = grad_ref[...]
    dr = grad + norm_back(d_m, normed, inv_std, vec[5:6, :])
    dr_ref[...] = dr
    dz_ref[...] = dr.astype(BF16)
    sums_ref[0:1, :] = jnp.sum(dr, axis=0, keepdims=True)
    sums_ref[1:2, :] = jnp.sum(d_m * normed, axis=0, keepdims=True)
    sums_ref[2:3, :] = jnp.sum(d_m, axis=0, keepdims=True)
    sums_ref[3:4, :] = jnp.sum(grad, axis=0, keepdims=True)


def attn_back_body(
    sc, z0, z1, z2, z3, x0, x1, x2, x3, wa, q_ref, k_ref, v_ref, lse_ref,
    dqkv_ref, bias_ref, sums_ref, p0, p1, p2, p3, dctx_ref,
):
    cols = q_ref.shape[1]
    block = z0.shape[0]
    wo = wa[:, 3 * cols :]
    for s, ref in enumerate((z0, z1, z2, z3)):
        dctx_ref[s * block : (s + 1) * block, :] = mm(ref[...], wo).astype(BF16)
    mask = time_mask(sc[1])
    scale = HEAD_DIM ** (-0.5)
    for h in range(cols // HEAD_DIM):
        lanes = slice(h * HEAD_DIM, (h + 1) * HEAD_DIM)
        sum_q = jnp.zeros((1, HEAD_DIM), F32)
        sum_v = jnp.zeros((1, HEAD_DIM), F32)
        for seq in range(q_ref.shape[0] // SEQ_LEN):
            rows = slice(seq * SEQ_LEN, (seq + 1) * SEQ_LEN)
            q, k, v, dc = q_ref[rows, lanes], k_ref[rows, lanes], v_ref[rows, lanes], dctx_ref[rows, lanes]
            s = jnp.where(mask, mm(q, k, 1, 1) * scale, MASK_LOW)
            p = jnp.exp(s - lse_ref[rows, h : h + 1])
            d_v = mm(p.astype(BF16), dc, 0, 0)
            d_p = mm(dc, v, 1, 1)
            row = jnp.sum(p * d_p, axis=-1, keepdims=True)
            d_s = (p * (d_p - row) * scale).astype(BF16)
            d_q = mm(d_s, k)
            d_k = mm(d_s, q, 0, 0)
            sum_q = sum_q + jnp.sum(d_q, axis=0, keepdims=True)
            sum_v = sum_v + jnp.sum(d_v, axis=0, keepdims=True)
            for j, val in enumerate((d_q, d_k, d_v)):
                at = j * cols + h * HEAD_DIM
                dqkv_ref[rows, at : at + HEAD_DIM] = val.astype(BF16)
        bias_ref[0:1, lanes] = sum_q
        bias_ref[1:2, lanes] = sum_v
    wqkv = wa[:, : 3 * cols]
    gain = jnp.zeros((1, wa.shape[0]), F32)
    shift = jnp.zeros((1, wa.shape[0]), F32)
    for s, (x, out) in enumerate(((x0, p0), (x1, p1), (x2, p2), (x3, p3))):
        d_a = mm(dqkv_ref[s * block : (s + 1) * block, :], wqkv, 1, 1)
        gain = gain + jnp.sum(d_a * x[...].astype(F32), axis=0, keepdims=True)
        shift = shift + jnp.sum(d_a, axis=0, keepdims=True)
        out[...] = d_a.astype(out.dtype)
    sums_ref[0:1, :] = gain
    sums_ref[1:2, :] = shift


def attn_grad_body(a_ref, dqkv_ref, z0, z1, z2, z3, ctx_ref, g_ref):
    wide = dqkv_ref.shape[1]
    g_ref[:, :wide] = mm(a_ref[...], dqkv_ref[...], 0, 0).astype(BF16)
    z = jnp.concatenate([z0[...], z1[...], z2[...], z3[...]], axis=0)
    g_ref[:, wide:] = mm(z, ctx_ref[...], 0, 0).astype(BF16)


def last_body(x_ref, p0, r1, r2, r3, dr_ref, vec, out_ref):
    d_a = p0[...] + (r1[...].astype(F32) + r2[...].astype(F32) + r3[...].astype(F32))
    normed, inv_std = norm_rows(x_ref[...])
    out_ref[...] = dr_ref[...] + norm_back(d_a, normed, inv_std, vec[0:1, :])


def swap(value, axis, size, step):
    return lax.ppermute(value, axis, [(i, i ^ step) for i in range(size)])


def tp_gather(value):
    far = {s: swap(value, "tensor", TP, s) for s in (3, 2, 1)}
    return [value, far[1], far[2], far[3]]


def tp_send(parts):
    far = {s: swap(parts[s], "tensor", TP, s) for s in (3, 2, 1)}
    return [parts[0], far[1], far[2], far[3]]


def dp_gather(shard, count, index):
    if count != 8:
        return lax.all_gather(shard, "dp", axis=0, tiled=True)
    rows, cols = shard.shape
    far = {s: swap(shard, "dp", count, 2 * s) for s in (3, 2, 1)}
    chips = jnp.stack([shard, far[1], far[2], far[3]]).reshape(2, 2, rows, cols)
    other = swap(chips, "dp", count, 1)
    both = jnp.where(
        index % 2 == 1, jnp.stack([other, chips], axis=2), jnp.stack([chips, other], axis=2)
    )
    both = jnp.where((index // 2) % 2 == 1, both[:, ::-1], both)
    both = jnp.where(index // 4 == 1, both[::-1], both)
    return both.reshape(count * rows, cols)


def dp_scatter(grad, count, index):
    if count != 8:
        return lax.psum_scatter(grad, "dp", scatter_dimension=0, tiled=True).astype(F32)
    rows = grad.shape[0] // count
    blocks = grad.reshape(4, 2, rows, grad.shape[1])
    core, chip = index % 2, index // 2
    got = swap(lax.dynamic_index_in_dim(blocks, 1 - core, 1, False), "dp", count, 1)
    mine = lax.dynamic_index_in_dim(blocks, core, 1, False).astype(F32) + got.astype(F32)
    low = mine.astype(BF16)
    total = lax.dynamic_index_in_dim(mine, chip, 0, False)
    for s in (3, 2, 1):
        total = total + swap(
            lax.dynamic_index_in_dim(low, chip ^ s, 0, False), "dp", count, 2 * s
        ).astype(F32)
    return total


def sum_all(table, count):
    if count != 8:
        return lax.psum(table, ("dp", "tensor"))
    table = table + swap(table, "dp", count, 1)
    table = table + sum(swap(table, "dp", count, 2 * s) for s in (1, 2, 3))
    return table + sum(swap(table, "tensor", TP, s) for s in (1, 2, 3))


def after(value, *others):
    return lax.optimization_barrier((value,) + tuple(others))[0]


def shards(inputs, qkv_weight, out_weight, fc_weight, proj_weight, vectors, out_grad):
    block, width = inputs.shape
    count = block * TP
    n_dp = lax.axis_size("dp")
    cols = qkv_weight.shape[3]
    hid = fc_weight.shape[2]
    part = lax.axis_index("tensor")
    index = lax.axis_index("dp")
    scalars = jnp.stack([part, part % 2]).astype(jnp.int32)
    blk = (block, width)

    xhat, dy = call(first_body, [(blk, BF16), (blk, BF16)], name="first")(inputs, out_grad)

    own = vectors.shape[2]
    place = index * TP + part
    spread = (
        lax.broadcasted_iota(jnp.int32, (own, width), 1)
        == place * own + lax.broadcasted_iota(jnp.int32, (own, width), 0)
    ).astype(F32)
    vec = sum_all(jnp.dot(vectors[0], spread, precision=lax.Precision.HIGHEST), n_dp)

    pack_a = jnp.concatenate([qkv_weight[0].reshape(-1, 3 * cols), out_weight[0].T], axis=1)
    pack_b = jnp.concatenate([fc_weight[0], proj_weight[0].T], axis=1)
    xs = tp_gather(xhat)
    wa = dp_gather(pack_a, n_dp, index)
    ds = tp_gather(after(dy, *xs))
    wb = dp_gather(after(pack_b, wa), n_dp, index)

    parts_out = [(blk, F32)] + [(blk, BF16)] * 3
    low = lambda n: ((count, n), BF16)
    res = call(
        attn_fwd_body,
        [low(width), low(cols), low(cols), low(cols), ((count, 128), F32), low(cols)] + parts_out,
        scalars, "attn_fwd",
    )(*xs, wa, vec)
    a_rows, q, k, v, lse, ctx = res[:6]
    resid1, m_own = call(norm2_body, [(blk, F32), (blk, BF16)], name="norm2")(
        inputs, *tp_send(res[6:]), vec
    )
    ms = tp_gather(m_own)
    res = call(
        mlp_body, [low(hid), low(hid), ((1, hid), F32)] + parts_out + parts_out, scalars, "mlp"
    )(*ms, *ds, wb, vec)
    h, du, g_bf = res[:3]
    out_parts, dm_parts = res[3:7], res[7:]
    dm = tp_send(dm_parts)
    (grad_b,) = call(mlp_grad_body, [((width, 2 * hid), BF16)], name="mlp_grad")(*ms, *ds, h, du)
    sum_b = dp_scatter(grad_b, n_dp, index)
    dr1, dz, sums2 = call(
        norm2_back_body, [(blk, F32), (blk, BF16), ((4, width), F32)], name="norm2_back"
    )(resid1, *dm, out_grad, vec)
    zs = tp_gather(dz)
    res = call(
        attn_back_body,
        [low(3 * cols), ((2, cols), F32), ((2, width), F32)] + parts_out,
        scalars, "attn_back", scratch=[pltpu.VMEM((count, cols), BF16)],
    )(*zs, *xs, wa, q, k, v, lse)
    dqkv, bias_sums, sums1 = res[:3]
    da = tp_send(res[3:])
    out_far = tp_send([out_parts[0]] + [after(p, *zs) for p in out_parts[1:]])
    outputs = resid1 + (
        out_far[0] + (out_far[1].astype(F32) + out_far[2].astype(F32) + out_far[3].astype(F32))
    ) + vec[7]

    row_q = lax.dynamic_update_slice_in_dim(jnp.zeros((1, width), F32), bias_sums[0:1], part * cols, 1)
    row_v = lax.dynamic_update_slice_in_dim(jnp.zeros((1, width), F32), bias_sums[1:2], part * cols, 1)
    bf_rows = jnp.where(lax.broadcasted_iota(jnp.int32, (TP, 1), 0) == part, g_bf, 0.0)
    table = jnp.concatenate([sums1, row_q, row_v, sums2, bf_rows], axis=0)
    (grad_a,) = call(attn_grad_body, [((width, 4 * cols), BF16)], name="attn_grad")(
        a_rows, dqkv, *zs, ctx
    )
    sum_a = dp_scatter(grad_a, n_dp, index)
    vec_sum = sum_all(table, n_dp)
    vector_grad = lax.dot_general(
        vec_sum, spread, (((1,), (1,)), ((), ())), precision=lax.Precision.HIGHEST
    )
    (input_grad,) = call(last_body, [(blk, F32)], name="last")(inputs, *da, dr1, vec)
    return (
        outputs,
        input_grad,
        sum_a[:, : 3 * cols].reshape(1, -1, 3, cols),
        sum_a[:, 3 * cols :].T[None],
        sum_b[:, :hid][None],
        sum_b[:, hid:].T[None],
        vector_grad[None],
    )


def solution(mesh):
    rows = P(("dp", "tensor"), None)
    weights = (
        P(None, "dp", None, "tensor"),
        P(None, "tensor", "dp"),
        P(None, "dp", "tensor"),
        P(None, "tensor", "dp"),
        P(None, None, ("dp", "tensor")),
    )
    return jax.shard_map(
        shards,
        mesh=mesh,
        in_specs=(rows,) + weights + (rows,),
        out_specs=(rows, rows) + weights,
        check_vma=False,
    )
```
